32 devices in a mesh: band: 16 (over z, x, core), ga: 2 (over y).
Axes of the slice: x: 2, y: 2, z: 4, core: 2. Of those that a mesh axis runs over, the one named last changes fastest.
Arguments:
- psi: float32 [8192, 8192], P('ga', 'band'), may hold values from -6 to 6
- tiles: float32 [16, 3, 512, 512], P('band', None, 'ga'), may hold values from -0.1875 to 0.1875
- half_width: int32 [1], replicated, may hold values from 384 to 512
Outputs:
- rotated: float32 [8192, 8192], P('ga', 'band')
The draws below stay inside these ranges and needn't reach their ends.
All inputs are finite; a program needn't handle non-finite values.
Results may differ from the reference program's by a relative error of at most 0.0001.
Values sent between devices are 32-bit elements; how exact they have to be, the bound alone decides.
A program may use at most 128 MiB of HBM per device.

```python
import jax
import jax.numpy as jnp
from jax import lax

NB = 8192
HALF = 512
BB = 512
REACH = 1
GV = 8192
N_BAND = 16


def block_scale(key, shape, split, smallest, top_value):
    level = 1.0
    for axis_at, parts in split:
        steps = jax.random.uniform(jax.random.fold_in(jax.random.fold_in(key, 6), axis_at), (parts,), jnp.float32, smallest / len(split), top_value / len(split))
        level = level * jnp.repeat(jnp.exp(steps), shape[axis_at] // parts).reshape((-1,) + (1,) * (len(shape) - 1 - axis_at))
    return level


def gaussian(own_key, dims, scale, most, cuts=(), held_as=jnp.bfloat16):
    array = scale * jax.random.normal(own_key, dims, jnp.float32)
    if cuts:
        array = array * block_scale(own_key, dims, cuts, -0.22, 0.18)
    return jnp.clip(array, -most, most).astype(held_as)


def setup_inputs(seed: int = 0) -> dict:
    key_list = jax.random.split(jax.random.key(seed), 4)
    return {
        "psi": gaussian(key_list[0], (GV, NB), 1.0, 6.0, ((0, 2), (1, 16)), jnp.float32),
        "tiles": gaussian(key_list[1], (N_BAND, 2 * REACH + 1, BB, BB), (2 * HALF) ** -0.5, 0.1875, ((0, 16), (2, 2)), jnp.float32),
        "half_width": jax.random.randint(key_list[2], (1,), HALF * 3 // 4, HALF + 1).astype(jnp.int32),
    }


def band_mask(span, width, half_width):
    reach = (span - 1) // 2
    index = jnp.arange(width).astype(jnp.int32)
    shifts = (jnp.arange(span).astype(jnp.int32) - reach) * width
    offsets = shifts[:, None, None] + index[None, :, None] - index[None, None, :]
    return (jnp.abs(offsets) <= half_width[0]).astype(jnp.float32)


def reference(psi, tiles, half_width):
    rows = psi.shape[0]
    blocks_count, span, width = tiles.shape[0], tiles.shape[1], tiles.shape[2]
    reach = (span - 1) // 2
    masked = tiles * band_mask(span, width, half_width)[None]
    blocks = psi.reshape(rows, blocks_count, width)
    padded = jnp.pad(blocks, ((0, 0), (reach, reach), (0, 0)))
    result = jnp.zeros((rows, blocks_count, width), jnp.float32)
    for k in range(span):
        panel = padded[:, k:k + blocks_count, :]
        result = result + jnp.einsum("gjb,jbc->gjc", panel, masked[:, k], precision=lax.Precision.HIGHEST)
    return result.reshape(rows, blocks_count * width)
```

```python
import functools

import jax
import jax.numpy as jnp
from jax import lax
from jax.experimental import pallas as pl
from jax.experimental.pallas import tpu as pltpu
from jax.sharding import PartitionSpec as P

MESH = pl.DeviceIdType.MESH
CHUNKS = 16


def split(x):
    high = x.astype(jnp.bfloat16)
    return high, (x - high.astype(jnp.float32)).astype(jnp.bfloat16)


def product(x, high, low):
    x_high, x_low = split(x)
    dot = functools.partial(jnp.dot, preferred_element_type=jnp.float32)
    return dot(x_high, high) + (dot(x_high, low) + dot(x_low, high))


def kernel(n, n_ga, plane, hw_ref, psi, tiles, out, own, near, relay, raw, high, low,
           own_sem, tile_send, tile_recv, send, recv, relay_send, relay_recv, forward_send):
    me = lax.axis_index("band")
    ga = lax.axis_index("ga")
    rows, width = psi.shape
    span, part = tiles.shape[1], tiles.shape[2]
    reach = (span - 1) // 2
    chunk = rows // CHUNKS
    planes = n // plane
    relays = plane >= 4 and planes > 1
    moves = [s * m for m in range(1, reach + 1) for s in (1, -1)]
    at, last = lax.rem(me, plane), lax.div(me, plane)

    peers = []
    for move in moves:
        there = me + move
        peers.append(((there >= 0) & (there < n), there))
        back = me - move
        peers.append(((back >= 0) & (back < n), back))
    up_src = (at == plane - 1) & (last < planes - 1)
    up_mid = (at == 0) & (last < planes - 1)
    up_dst = (at == 0) & (last > 0)
    down_src = (at == 0) & (last > 0)
    down_mid = (at == plane - 2) & (last > 0)
    down_dst = (at == plane - 1) & (last < planes - 1)
    up_mid_of_src = me - (plane - 1)
    down_mid_of_src = me + (plane - 2)
    if relays:
        peers += [
            (up_src, me - (plane - 1)), (up_mid, me + (plane - 1)),
            (up_mid, me + plane), (up_dst, me - plane),
            (down_src, me + (plane - 2)), (down_mid, me - (plane - 2)),
            (down_mid, me - (plane - 1)), (down_dst, me + (plane - 1)),
        ]
    barrier = pltpu.get_barrier_semaphore()
    count = jnp.int32(n_ga - 1)
    for step in range(1, n_ga):
        pl.semaphore_signal(barrier, inc=1, device_id=(me, lax.rem(ga + step, n_ga)), device_id_type=MESH)
    for cond, peer in peers:
        @pl.when(cond)
        def _(peer=peer):
            pl.semaphore_signal(barrier, inc=1, device_id=(peer, ga), device_id_type=MESH)
        count = count + cond.astype(jnp.int32)
    pl.semaphore_wait(barrier, count)

    def block(c):
        return pl.ds(pl.multiple_of(c * chunk, chunk), chunk)

    def direct_copy(slot, move, c):
        return pltpu.make_async_remote_copy(
            psi.at[block(c)], near.at[slot, block(c)], send.at[slot, c], recv.at[slot, c],
            device_id=(me + move, ga), device_id_type=MESH)

    def relay_copy(slot, mid, c):
        return pltpu.make_async_remote_copy(
            psi.at[block(c)], relay.at[block(c)], send.at[slot, c], relay_recv.at[c],
            device_id=(mid, ga), device_id_type=MESH)

    def forward_copy(slot, to, c):
        return pltpu.make_async_remote_copy(
            relay.at[block(c)], near.at[slot, block(c)], forward_send.at[c], recv.at[slot, c],
            device_id=(to, ga), device_id_type=MESH)

    def goes_up(p, c):
        return lax.rem(c, planes) < planes - 1 - p

    def goes_down(p, c):
        return lax.rem(c, planes) < p

    def tile_copy(step):
        peer = lax.rem(ga + step, n_ga)
        return pltpu.make_async_remote_copy(
            tiles.at[0], raw.at[:, pl.ds(pl.multiple_of(ga * part, part), part), :],
            tile_send.at[step - 1], tile_recv.at[step - 1],
            device_id=(me, peer), device_id_type=MESH)

    for step in range(1, n_ga):
        tile_copy(step).start()

    def start(c, carry):
        for slot, move in enumerate(moves):
            there = me + move
            valid = (there >= 0) & (there < n)
            if relays and abs(move) == 1:
                src, mid = (up_src, up_mid_of_src) if move == 1 else (down_src, down_mid_of_src)
                via = src & (goes_up(last, c) if move == 1 else goes_down(last, c))

                @pl.when(via)
                def _():
                    relay_copy(slot, mid, c).start()
                valid = valid & jnp.logical_not(via)

            @pl.when(valid)
            def _():
                direct_copy(slot, move, c).start()
        return carry
    lax.fori_loop(0, CHUNKS, start, 0)

    own_tiles = pltpu.make_async_copy(
        tiles.at[0], raw.at[:, pl.ds(pl.multiple_of(ga * part, part), part), :], own_sem.at[1])
    own_tiles.start()
    own_psi = pltpu.make_async_copy(psi, own, own_sem.at[0])
    own_psi.start()
    own_tiles.wait()
    for step in range(1, n_ga):
        tile_copy(step).wait_recv()
    half = hw_ref[0]
    piece = min(width, 128)
    for k in range(span):
        for r in range(0, width, piece):
            row = lax.broadcasted_iota(jnp.int32, (piece, width), 0) + (r + (k - reach) * width)
            col = lax.broadcasted_iota(jnp.int32, (piece, width), 1)
            u = jnp.where(jnp.abs(row - col) <= half, raw[k, r:r + piece, :], 0.0)
            u_high, u_low = split(u)
            high[k, r:r + piece, :] = u_high
            low[k, r:r + piece, :] = u_low
    own_psi.wait()

    def centre(c, carry):
        out[block(c), :] = product(own[block(c), :], high[reach], low[reach])
        return carry
    lax.fori_loop(0, CHUNKS, centre, 0)

    def step(c, carry):
        if relays:
            @pl.when(up_mid & goes_up(last, c))
            def _():
                relay_copy(0, me, c).wait_recv()
                forward_copy(0, me + plane, c).start()

            @pl.when(down_mid & goes_down(last, c))
            def _():
                relay_copy(1, me, c).wait_recv()
                forward_copy(1, me - (plane - 1), c).start()
        for slot, move in enumerate(moves):
            back = me - move

            @pl.when((back >= 0) & (back < n))
            def _():
                direct_copy(slot, move, c).wait_recv()
                k = reach - move
                out[block(c), :] += product(near[slot, block(c), :], high[k], low[k])
        return carry
    lax.fori_loop(0, CHUNKS, step, 0)

    def finish(c, carry):
        for slot, move in enumerate(moves):
            there = me + move

            @pl.when((there >= 0) & (there < n))
            def _():
                direct_copy(slot, move, c).wait_send()
        if relays:
            @pl.when((up_mid & goes_up(last, c)) | (down_mid & goes_down(last, c)))
            def _():
                forward_copy(0, me, c).wait_send()
        return carry
    lax.fori_loop(0, CHUNKS, finish, 0)
    for step_ in range(1, n_ga):
        tile_copy(step_).wait_send()


def plane_size(mesh):
    axis = mesh.axis_names.index("band")
    line = mesh.devices.take(0, axis=1 - axis)
    coords = [getattr(d, "coords", None) for d in line]
    if coords[0] is None:
        return len(coords)
    return sum(c[2] == coords[0][2] for c in coords)


def solution(mesh):
    n, n_ga = mesh.shape["band"], mesh.shape["ga"]
    plane = plane_size(mesh)

    def on_device(psi, tiles, half_width):
        rows, width = psi.shape
        span = tiles.shape[1]
        f32, bf16 = jnp.float32, jnp.bfloat16
        dma = pltpu.SemaphoreType.DMA
        sides = span - 1
        return pl.pallas_call(
            functools.partial(kernel, n, n_ga, plane),
            out_shape=jax.ShapeDtypeStruct((rows, width), f32),
            in_specs=[
                pl.BlockSpec(memory_space=pltpu.SMEM),
                pl.BlockSpec(memory_space=pl.ANY),
                pl.BlockSpec(memory_space=pl.ANY),
            ],
            out_specs=pl.BlockSpec(memory_space=pltpu.VMEM),
            scratch_shapes=[
                pltpu.VMEM((rows, width), f32),
                pltpu.VMEM((sides, rows, width), f32),
                pltpu.VMEM((rows, width), f32),
                pltpu.VMEM((span, width, width), f32),
                pltpu.VMEM((span, width, width), bf16),
                pltpu.VMEM((span, width, width), bf16),
                dma((2,)),
                dma((n_ga - 1,)),
                dma((n_ga - 1,)),
                dma((sides, CHUNKS)),
                dma((sides, CHUNKS)),
                dma((CHUNKS,)),
                dma((CHUNKS,)),
                dma((CHUNKS,)),
            ],
            compiler_params=pltpu.CompilerParams(
                collective_id=0, has_side_effects=True, vmem_limit_bytes=60 * 2**20),
            name="rotate",
        )(half_width, psi, tiles)

    return jax.shard_map(
        on_device,
        mesh=mesh,
        in_specs=(P("ga", "band"), P("band", None, "ga", None), P()),
        out_specs=P("ga", "band"),
        check_vma=False,
    )
```

```python
import functools

import jax
import jax.numpy as jnp
from jax import lax
from jax.experimental import pallas as pl
from jax.experimental.pallas import tpu as pltpu
from jax.sharding import PartitionSpec as P

MESH = pl.DeviceIdType.MESH
CHUNKS = 16
EDGE_CHUNKS = 8
LANES = 128
LEVELS = 4


def split(x):
    high = x.astype(jnp.bfloat16)
    return high, (x - high.astype(jnp.float32)).astype(jnp.bfloat16)


def product(x, high, low):
    x_high, x_low = split(x)
    dot = functools.partial(jnp.dot, preferred_element_type=jnp.float32)
    return dot(x_high, high) + (dot(x_high, low) + dot(x_low, high))


def kernel(n, n_ga, plane, edge, hw_ref, psi, tiles, out, own, near, relay, raw, high, low,
           edge_own, edge_near, edge_relay, own_sem, tile_send, tile_recv, send, recv, relay_recv,
           forward_send, edge_send, edge_recv, edge_relay_recv, edge_forward_send):
    me = lax.axis_index("band")
    ga = lax.axis_index("ga")
    rows, width = psi.shape
    span, part = tiles.shape[1], tiles.shape[2]
    reach = (span - 1) // 2
    chunk = rows // CHUNKS
    edge_rows = rows // EDGE_CHUNKS
    edge_at = (LANES - edge, 0)
    planes = n // plane
    relays = plane >= 4 and planes > 1
    moves = [s * m for m in range(1, reach + 1) for s in (1, -1)]
    at, last = lax.rem(me, plane), lax.div(me, plane)

    peers = []
    for move in moves:
        there = me + move
        peers.append(((there >= 0) & (there < n), there))
        back = me - move
        peers.append(((back >= 0) & (back < n), back))
    up_src = (at == plane - 1) & (last < planes - 1)
    up_mid = (at == 0) & (last < planes - 1)
    up_dst = (at == 0) & (last > 0)
    down_src = (at == 0) & (last > 0)
    down_mid = (at == plane - 2) & (last > 0)
    down_dst = (at == plane - 1) & (last < planes - 1)
    up_mid_of_src = me - (plane - 1)
    down_mid_of_src = me + (plane - 2)
    if relays:
        peers += [
            (up_src, me - (plane - 1)), (up_mid, me + (plane - 1)),
            (up_mid, me + plane), (up_dst, me - plane),
            (down_src, me + (plane - 2)), (down_mid, me - (plane - 2)),
            (down_mid, me - (plane - 1)), (down_dst, me + (plane - 1)),
        ]
    barrier = pltpu.get_barrier_semaphore()
    count = jnp.int32(n_ga - 1)
    for step in range(1, n_ga):
        pl.semaphore_signal(barrier, inc=1, device_id=(me, lax.rem(ga + step, n_ga)), device_id_type=MESH)
    for cond, peer in peers:
        @pl.when(cond)
        def _(peer=peer):
            pl.semaphore_signal(barrier, inc=1, device_id=(peer, ga), device_id_type=MESH)
        count = count + cond.astype(jnp.int32)
    pl.semaphore_wait(barrier, count)

    def block(c):
        return pl.ds(pl.multiple_of(c * chunk, chunk), chunk)

    def columns(slot, move):
        if abs(move) != reach:
            return pl.ds(0, width)
        return pl.ds(LANES if slot % 2 == 0 else 0, width - LANES)

    def direct_copy(slot, move, c):
        at_ = (block(c), columns(slot, move))
        return pltpu.make_async_remote_copy(
            psi.at[at_], near.at[(slot, *at_)], send.at[slot, c], recv.at[slot, c],
            device_id=(me + move, ga), device_id_type=MESH)

    def relay_copy(slot, mid, c):
        at_ = (block(c), columns(slot, moves[slot]))
        return pltpu.make_async_remote_copy(
            psi.at[at_], relay.at[at_], send.at[slot, c], relay_recv.at[c],
            device_id=(mid, ga), device_id_type=MESH)

    def forward_copy(slot, to, c):
        at_ = (block(c), columns(slot, moves[slot]))
        return pltpu.make_async_remote_copy(
            relay.at[at_], near.at[(slot, *at_)], forward_send.at[c], recv.at[slot, c],
            device_id=(to, ga), device_id_type=MESH)

    def edge_direct(side, move, c):
        at_ = pl.ds(edge_at[side], edge)
        return pltpu.make_async_remote_copy(
            edge_own.at[side, c, at_], edge_near.at[side, c, at_],
            edge_send.at[side, c], edge_recv.at[side, c],
            device_id=(me + move, ga), device_id_type=MESH)

    def edge_relayed(side, mid, c):
        at_ = pl.ds(edge_at[side], edge)
        return pltpu.make_async_remote_copy(
            edge_own.at[side, c, at_], edge_relay.at[c, at_],
            edge_send.at[side, c], edge_relay_recv.at[c],
            device_id=(mid, ga), device_id_type=MESH)

    def edge_forward(side, to, c):
        at_ = pl.ds(edge_at[side], edge)
        return pltpu.make_async_remote_copy(
            edge_relay.at[c, at_], edge_near.at[side, c, at_],
            edge_forward_send.at[c], edge_recv.at[side, c],
            device_id=(to, ga), device_id_type=MESH)

    def goes_up(p, c):
        return lax.rem(c, planes) < planes - 1 - p

    def goes_down(p, c):
        return lax.rem(c, planes) < p

    def tile_copy(step):
        peer = lax.rem(ga + step, n_ga)
        return pltpu.make_async_remote_copy(
            tiles.at[0], raw.at[:, pl.ds(pl.multiple_of(ga * part, part), part), :],
            tile_send.at[step - 1], tile_recv.at[step - 1],
            device_id=(me, peer), device_id_type=MESH)

    for step in range(1, n_ga):
        tile_copy(step).start()

    def send_from(slot, move, c, straight, through):
        there = me + move
        valid = (there >= 0) & (there < n)
        if relays and abs(move) == 1:
            src, mid = (up_src, up_mid_of_src) if move == 1 else (down_src, down_mid_of_src)
            via = src & (goes_up(last, c) if move == 1 else goes_down(last, c))

            @pl.when(via)
            def _():
                through(slot, mid, c).start()
            valid = valid & jnp.logical_not(via)

        @pl.when(valid)
        def _():
            straight(slot, move, c).start()

    def start(c, carry):
        for slot, move in enumerate(moves):
            send_from(slot, move, c, direct_copy, relay_copy)
        return carry
    lax.fori_loop(0, CHUNKS, start, 0)

    own_tiles = pltpu.make_async_copy(
        tiles.at[0], raw.at[:, pl.ds(pl.multiple_of(ga * part, part), part), :], own_sem.at[1])
    own_tiles.start()
    own_psi = pltpu.make_async_copy(psi, own, own_sem.at[0])
    own_psi.start()
    own_tiles.wait()
    for step in range(1, n_ga):
        tile_copy(step).wait_recv()
    half = hw_ref[0]
    piece = min(width, 128)
    for k in range(span):
        for r in range(0, width, piece):
            row = lax.broadcasted_iota(jnp.int32, (piece, width), 0) + (r + (k - reach) * width)
            col = lax.broadcasted_iota(jnp.int32, (piece, width), 1)
            u = jnp.where(jnp.abs(row - col) <= half, raw[k, r:r + piece, :], 0.0)
            u_high, u_low = split(u)
            high[k, r:r + piece, :] = u_high
            low[k, r:r + piece, :] = u_low
    own_psi.wait()

    def edge_block(c):
        return pl.ds(pl.multiple_of(c * edge_rows, edge_rows), edge_rows)

    def turn(c, carry):
        edge_own[0, c] = jnp.transpose(own[edge_block(c), 0:LANES])
        edge_own[1, c] = jnp.transpose(own[edge_block(c), width - LANES:width])
        if edge < LANES:
            blank = jnp.zeros((LANES - edge, edge_rows), jnp.float32)
            edge_near[0, c, 0:LANES - edge, :] = blank
            edge_near[1, c, edge:LANES, :] = blank
        return carry
    lax.fori_loop(0, EDGE_CHUNKS, turn, 0)

    def centre(c, carry):
        out[block(c), :] = product(own[block(c), :], high[reach], low[reach])
        return carry
    lax.fori_loop(0, CHUNKS, centre, 0)

    outer = (reach, -reach)

    def edge_start(c, carry):
        for side, move in enumerate(outer):
            send_from(side, move, c, edge_direct, edge_relayed)
        return carry
    lax.fori_loop(0, EDGE_CHUNKS, edge_start, 0)

    def pass_on(c, arrive, forward):
        @pl.when(up_mid & goes_up(last, c))
        def _():
            arrive(0, me, c).wait_recv()
            forward(0, me + plane, c).start()

        @pl.when(down_mid & goes_down(last, c))
        def _():
            arrive(1, me, c).wait_recv()
            forward(1, me - (plane - 1), c).start()

    def step(c, carry):
        if relays:
            pass_on(c, relay_copy, forward_copy)
        for slot, move in enumerate(moves):
            back = me - move

            @pl.when((back >= 0) & (back < n))
            def _():
                direct_copy(slot, move, c).wait_recv()
                k = reach - move
                cols = columns(slot, move)
                cols = slice(cols.start, cols.start + cols.size)
                out[block(c), :] += product(near[slot, block(c), cols], high[k, cols, :], low[k, cols, :])
        return carry
    lax.fori_loop(0, CHUNKS, step, 0)

    def edge_step(c, carry):
        if relays and reach == 1:
            pass_on(c, edge_relayed, edge_forward)
        for side, move in enumerate(outer):
            back = me - move

            @pl.when((back >= 0) & (back < n))
            def _():
                edge_direct(side, move, c).wait_recv()
                k = reach - move
                cols = slice(0, LANES) if side == 0 else slice(width - LANES, width)
                x = jnp.transpose(edge_near[side, c])
                out[edge_block(c), :] += product(x, high[k, cols, :], low[k, cols, :])
        return carry
    lax.fori_loop(0, EDGE_CHUNKS, edge_step, 0)

    def finish(c, carry):
        for slot, move in enumerate(moves):
            there = me + move

            @pl.when((there >= 0) & (there < n))
            def _():
                direct_copy(slot, move, c).wait_send()
        if relays:
            @pl.when((up_mid & goes_up(last, c)) | (down_mid & goes_down(last, c)))
            def _():
                forward_copy(0, me, c).wait_send()
        return carry
    lax.fori_loop(0, CHUNKS, finish, 0)

    def edge_finish(c, carry):
        for side, move in enumerate(outer):
            there = me + move

            @pl.when((there >= 0) & (there < n))
            def _():
                edge_direct(side, move, c).wait_send()
        if relays and reach == 1:
            @pl.when((up_mid & goes_up(last, c)) | (down_mid & goes_down(last, c)))
            def _():
                edge_forward(0, me, c).wait_send()
        return carry
    lax.fori_loop(0, EDGE_CHUNKS, edge_finish, 0)
    for step_ in range(1, n_ga):
        tile_copy(step_).wait_send()


def plane_size(mesh):
    axis = mesh.axis_names.index("band")
    line = mesh.devices.take(0, axis=1 - axis)
    coords = [getattr(d, "coords", None) for d in line]
    if coords[0] is None:
        return len(coords)
    return sum(c[2] == coords[0][2] for c in coords)


def solution(mesh):
    n, n_ga = mesh.shape["band"], mesh.shape["ga"]
    plane = plane_size(mesh)

    def rotate(level, psi, tiles, half_width):
        rows, width = psi.shape
        span = tiles.shape[1]
        sides = span - 1
        edge = LANES * (level + 1) // LEVELS
        f32, bf16 = jnp.float32, jnp.bfloat16
        dma = pltpu.SemaphoreType.DMA
        edge_shape = (EDGE_CHUNKS, LANES, rows // EDGE_CHUNKS)
        return pl.pallas_call(
            functools.partial(kernel, n, n_ga, plane, edge),
            out_shape=pltpu.VMEM((rows, width), f32),
            in_specs=[
                pl.BlockSpec(memory_space=pltpu.SMEM),
                pl.BlockSpec(memory_space=pl.ANY),
                pl.BlockSpec(memory_space=pl.ANY),
            ],
            out_specs=pl.BlockSpec(memory_space=pltpu.VMEM),
            scratch_shapes=[
                pltpu.VMEM((rows, width), f32),
                pltpu.VMEM((sides, rows, width), f32),
                pltpu.VMEM((rows, width), f32),
                pltpu.VMEM((span, width, width), f32),
                pltpu.VMEM((span, width, width), bf16),
                pltpu.VMEM((span, width, width), bf16),
                pltpu.VMEM((2, *edge_shape), f32),
                pltpu.VMEM((2, *edge_shape), f32),
                pltpu.VMEM(edge_shape, f32),
                dma((2,)),
                dma((n_ga - 1,)),
                dma((n_ga - 1,)),
                dma((sides, CHUNKS)),
                dma((sides, CHUNKS)),
                dma((CHUNKS,)),
                dma((CHUNKS,)),
                dma((2, EDGE_CHUNKS)),
                dma((2, EDGE_CHUNKS)),
                dma((EDGE_CHUNKS,)),
                dma((EDGE_CHUNKS,)),
            ],
            compiler_params=pltpu.CompilerParams(
                collective_id=level, has_side_effects=True, vmem_limit_bytes=52 * 2**20),
            name=f"rotate_{edge}",
        )(half_width, psi, tiles)

    def on_device(psi, tiles, half_width):
        width = psi.shape[1]
        reach = (tiles.shape[1] - 1) // 2
        beyond = half_width[0] - (reach * width - LANES + 1)
        level = lax.shift_right_arithmetic(beyond, (LANES // LEVELS).bit_length() - 1)
        branches = [functools.partial(rotate, i) for i in range(LEVELS)]
        return lax.switch(level, branches, psi, tiles, half_width)

    return jax.shard_map(
        on_device,
        mesh=mesh,
        in_specs=(P("ga", "band"), P("band", None, "ga", None), P()),
        out_specs=P("ga", "band"),
        check_vma=False,
    )
```

```python
import functools

import jax
import jax.numpy as jnp
from jax import lax
from jax.experimental import pallas as pl
from jax.experimental.pallas import tpu as pltpu
from jax.sharding import PartitionSpec as P

MESH = pl.DeviceIdType.MESH
CHUNKS = 8
EDGE_CHUNKS = 4
LANES = 128
LEVELS = 8
AHEAD = 1
EDGE_AHEAD = 2


def split(x):
    high = x.astype(jnp.bfloat16)
    return high, (x - high.astype(jnp.float32)).astype(jnp.bfloat16)


def product(x, high, low):
    x_high, x_low = split(x)
    dot = functools.partial(jnp.dot, preferred_element_type=jnp.float32)
    return dot(x_high, high) + (dot(x_high, low) + dot(x_low, high))


def kernel(n, n_ga, plane, edge, hw_ref, psi, tiles, out, own, near, relay, raw, high, low,
           edge_own, edge_near, edge_relay, own_sem, tile_send, tile_recv, send, recv, relay_recv,
           forward_send, edge_send, edge_recv, edge_relay_recv, edge_forward_send):
    me = lax.axis_index("band")
    ga = lax.axis_index("ga")
    rows, width = psi.shape
    span, part = tiles.shape[1], tiles.shape[2]
    reach = (span - 1) // 2
    chunk = rows // CHUNKS
    edge_rows = rows // EDGE_CHUNKS
    edge_at = (LANES - edge, 0)
    planes = n // plane
    relays = plane >= 4 and planes > 1
    moves = [s * m for m in range(1, reach + 1) for s in (1, -1)]
    at, last = lax.rem(me, plane), lax.div(me, plane)

    peers = []
    for move in moves:
        there = me + move
        peers.append(((there >= 0) & (there < n), there))
        back = me - move
        peers.append(((back >= 0) & (back < n), back))
    up_src = (at == plane - 1) & (last < planes - 1)
    up_mid = (at == 0) & (last < planes - 1)
    up_dst = (at == 0) & (last > 0)
    down_src = (at == 0) & (last > 0)
    down_mid = (at == plane - 2) & (last > 0)
    down_dst = (at == plane - 1) & (last < planes - 1)
    up_mid_of_src = me - (plane - 1)
    down_mid_of_src = me + (plane - 2)
    if relays:
        peers += [
            (up_src, me - (plane - 1)), (up_mid, me + (plane - 1)),
            (up_mid, me + plane), (up_dst, me - plane),
            (down_src, me + (plane - 2)), (down_mid, me - (plane - 2)),
            (down_mid, me - (plane - 1)), (down_dst, me + (plane - 1)),
        ]
    barrier = pltpu.get_barrier_semaphore()
    count = jnp.int32(n_ga - 1)
    for step in range(1, n_ga):
        pl.semaphore_signal(barrier, inc=1, device_id=(me, lax.rem(ga + step, n_ga)), device_id_type=MESH)
    for cond, peer in peers:
        @pl.when(cond)
        def _(peer=peer):
            pl.semaphore_signal(barrier, inc=1, device_id=(peer, ga), device_id_type=MESH)
        count = count + cond.astype(jnp.int32)
    pl.semaphore_wait(barrier, count)

    def block(c):
        return pl.ds(pl.multiple_of(c * chunk, chunk), chunk)

    def columns(slot, move):
        if abs(move) != reach:
            return pl.ds(0, width)
        return pl.ds(LANES if slot % 2 == 0 else 0, width - LANES)

    def direct_copy(slot, move, c):
        at_ = (block(c), columns(slot, move))
        return pltpu.make_async_remote_copy(
            psi.at[at_], near.at[(slot, *at_)], send.at[slot, c], recv.at[slot, c],
            device_id=(me + move, ga), device_id_type=MESH)

    def relay_copy(slot, mid, c):
        at_ = (block(c), columns(slot, moves[slot]))
        return pltpu.make_async_remote_copy(
            psi.at[at_], relay.at[at_], send.at[slot, c], relay_recv.at[c],
            device_id=(mid, ga), device_id_type=MESH)

    def forward_copy(slot, to, c):
        at_ = (block(c), columns(slot, moves[slot]))
        return pltpu.make_async_remote_copy(
            relay.at[at_], near.at[(slot, *at_)], forward_send.at[c], recv.at[slot, c],
            device_id=(to, ga), device_id_type=MESH)

    def edge_direct(side, move, c):
        at_ = pl.ds(edge_at[side], edge)
        return pltpu.make_async_remote_copy(
            edge_own.at[side, c, at_], edge_near.at[side, c, at_],
            edge_send.at[side, c], edge_recv.at[side, c],
            device_id=(me + move, ga), device_id_type=MESH)

    def edge_relayed(side, mid, c):
        at_ = pl.ds(edge_at[side], edge)
        return pltpu.make_async_remote_copy(
            edge_own.at[side, c, at_], edge_relay.at[c, at_],
            edge_send.at[side, c], edge_relay_recv.at[c],
            device_id=(mid, ga), device_id_type=MESH)

    def edge_forward(side, to, c):
        at_ = pl.ds(edge_at[side], edge)
        return pltpu.make_async_remote_copy(
            edge_relay.at[c, at_], edge_near.at[side, c, at_],
            edge_forward_send.at[c], edge_recv.at[side, c],
            device_id=(to, ga), device_id_type=MESH)

    def goes_up(p, c):
        return lax.rem(c, planes) < planes - 1 - p

    def goes_down(p, c):
        return lax.rem(c, planes) < p

    def tile_copy(step):
        peer = lax.rem(ga + step, n_ga)
        return pltpu.make_async_remote_copy(
            tiles.at[0], raw.at[:, pl.ds(pl.multiple_of(ga * part, part), part), :],
            tile_send.at[step - 1], tile_recv.at[step - 1],
            device_id=(me, peer), device_id_type=MESH)

    for step in range(1, n_ga):
        tile_copy(step).start()

    def send_from(slot, move, c, straight, through):
        there = me + move
        valid = (there >= 0) & (there < n)
        if relays and abs(move) == 1:
            src, mid = (up_src, up_mid_of_src) if move == 1 else (down_src, down_mid_of_src)
            via = src & (goes_up(last, c) if move == 1 else goes_down(last, c))

            @pl.when(via)
            def _():
                through(slot, mid, c).start()
            valid = valid & jnp.logical_not(via)

        @pl.when(valid)
        def _():
            straight(slot, move, c).start()

    def start(c, carry):
        for slot, move in enumerate(moves):
            send_from(slot, move, c, direct_copy, relay_copy)
        return carry
    lax.fori_loop(0, CHUNKS, start, 0)

    own_tiles = pltpu.make_async_copy(
        tiles.at[0], raw.at[:, pl.ds(pl.multiple_of(ga * part, part), part), :], own_sem.at[1])
    own_tiles.start()
    own_psi = pltpu.make_async_copy(psi, own, own_sem.at[0])
    own_psi.start()
    own_tiles.wait()
    for step in range(1, n_ga):
        tile_copy(step).wait_recv()
    half = hw_ref[0]
    piece = min(width, 128)
    for k in range(span):
        for r in range(0, width, piece):
            row = lax.broadcasted_iota(jnp.int32, (piece, width), 0) + (r + (k - reach) * width)
            col = lax.broadcasted_iota(jnp.int32, (piece, width), 1)
            u = jnp.where(jnp.abs(row - col) <= half, raw[k, r:r + piece, :], 0.0)
            u_high, u_low = split(u)
            high[k, r:r + piece, :] = u_high
            low[k, r:r + piece, :] = u_low
    own_psi.wait()

    def edge_block(c):
        return pl.ds(pl.multiple_of(c * edge_rows, edge_rows), edge_rows)

    def turn(c, carry):
        edge_own[0, c] = jnp.transpose(own[edge_block(c), 0:LANES])
        edge_own[1, c] = jnp.transpose(own[edge_block(c), width - LANES:width])
        if edge < LANES:
            blank = jnp.zeros((LANES - edge, edge_rows), jnp.float32)
            edge_near[0, c, 0:LANES - edge, :] = blank
            edge_near[1, c, edge:LANES, :] = blank
        return carry
    lax.fori_loop(0, EDGE_CHUNKS, turn, 0)

    def centre(c, carry):
        out[block(c), :] = product(own[block(c), :], high[reach], low[reach])
        return carry
    lax.fori_loop(0, CHUNKS, centre, 0)

    outer = (reach, -reach)

    def edge_start(c, carry):
        for side, move in enumerate(outer):
            send_from(side, move, c, edge_direct, edge_relayed)
        return carry
    lax.fori_loop(0, EDGE_CHUNKS, edge_start, 0)

    def pass_on(c, arrive, forward):
        @pl.when(up_mid & goes_up(last, c))
        def _():
            arrive(0, me, c).wait_recv()
            forward(0, me + plane, c).start()

        @pl.when(down_mid & goes_down(last, c))
        def _():
            arrive(1, me, c).wait_recv()
            forward(1, me - (plane - 1), c).start()

    if relays:
        for c in range(AHEAD):
            pass_on(jnp.int32(c), relay_copy, forward_copy)

    def step(c, carry):
        if relays:
            @pl.when(c + AHEAD < CHUNKS)
            def _():
                pass_on(c + AHEAD, relay_copy, forward_copy)
        for slot, move in enumerate(moves):
            back = me - move

            @pl.when((back >= 0) & (back < n))
            def _():
                direct_copy(slot, move, c).wait_recv()
                k = reach - move
                cols = columns(slot, move)
                cols = slice(cols.start, cols.start + cols.size)
                out[block(c), :] += product(near[slot, block(c), cols], high[k, cols, :], low[k, cols, :])
        return carry
    lax.fori_loop(0, CHUNKS, step, 0)

    if relays and reach == 1:
        for c in range(EDGE_AHEAD):
            pass_on(jnp.int32(c), edge_relayed, edge_forward)

    def edge_step(c, carry):
        if relays and reach == 1:
            @pl.when(c + EDGE_AHEAD < EDGE_CHUNKS)
            def _():
                pass_on(c + EDGE_AHEAD, edge_relayed, edge_forward)
        for side, move in enumerate(outer):
            back = me - move

            @pl.when((back >= 0) & (back < n))
            def _():
                edge_direct(side, move, c).wait_recv()
                k = reach - move
                cols = slice(0, LANES) if side == 0 else slice(width - LANES, width)
                x = jnp.transpose(edge_near[side, c])
                out[edge_block(c), :] += product(x, high[k, cols, :], low[k, cols, :])
        return carry
    lax.fori_loop(0, EDGE_CHUNKS, edge_step, 0)

    def finish(c, carry):
        for slot, move in enumerate(moves):
            there = me + move

            @pl.when((there >= 0) & (there < n))
            def _():
                direct_copy(slot, move, c).wait_send()
        if relays:
            @pl.when((up_mid & goes_up(last, c)) | (down_mid & goes_down(last, c)))
            def _():
                forward_copy(0, me, c).wait_send()
        return carry
    lax.fori_loop(0, CHUNKS, finish, 0)

    def edge_finish(c, carry):
        for side, move in enumerate(outer):
            there = me + move

            @pl.when((there >= 0) & (there < n))
            def _():
                edge_direct(side, move, c).wait_send()
        if relays and reach == 1:
            @pl.when((up_mid & goes_up(last, c)) | (down_mid & goes_down(last, c)))
            def _():
                edge_forward(0, me, c).wait_send()
        return carry
    lax.fori_loop(0, EDGE_CHUNKS, edge_finish, 0)
    for step_ in range(1, n_ga):
        tile_copy(step_).wait_send()


def plane_size(mesh):
    axis = mesh.axis_names.index("band")
    line = mesh.devices.take(0, axis=1 - axis)
    coords = [getattr(d, "coords", None) for d in line]
    if coords[0] is None:
        return len(coords)
    return sum(c[2] == coords[0][2] for c in coords)


def solution(mesh):
    n, n_ga = mesh.shape["band"], mesh.shape["ga"]
    plane = plane_size(mesh)

    def rotate(level, psi, tiles, half_width):
        rows, width = psi.shape
        span = tiles.shape[1]
        sides = span - 1
        edge = LANES * (level + 1) // LEVELS
        f32, bf16 = jnp.float32, jnp.bfloat16
        dma = pltpu.SemaphoreType.DMA
        edge_shape = (EDGE_CHUNKS, LANES, rows // EDGE_CHUNKS)
        return pl.pallas_call(
            functools.partial(kernel, n, n_ga, plane, edge),
            out_shape=pltpu.VMEM((rows, width), f32),
            in_specs=[
                pl.BlockSpec(memory_space=pltpu.SMEM),
                pl.BlockSpec(memory_space=pl.ANY),
                pl.BlockSpec(memory_space=pl.ANY),
            ],
            out_specs=pl.BlockSpec(memory_space=pltpu.VMEM),
            scratch_shapes=[
                pltpu.VMEM((rows, width), f32),
                pltpu.VMEM((sides, rows, width), f32),
                pltpu.VMEM((rows, width), f32),
                pltpu.VMEM((span, width, width), f32),
                pltpu.VMEM((span, width, width), bf16),
                pltpu.VMEM((span, width, width), bf16),
                pltpu.VMEM((2, *edge_shape), f32),
                pltpu.VMEM((2, *edge_shape), f32),
                pltpu.VMEM(edge_shape, f32),
                dma((2,)),
                dma((n_ga - 1,)),
                dma((n_ga - 1,)),
                dma((sides, CHUNKS)),
                dma((sides, CHUNKS)),
                dma((CHUNKS,)),
                dma((CHUNKS,)),
                dma((2, EDGE_CHUNKS)),
                dma((2, EDGE_CHUNKS)),
                dma((EDGE_CHUNKS,)),
                dma((EDGE_CHUNKS,)),
            ],
            compiler_params=pltpu.CompilerParams(
                collective_id=level, has_side_effects=True, vmem_limit_bytes=52 * 2**20),
            name=f"rotate_{edge}",
        )(half_width, psi, tiles)

    def on_device(psi, tiles, half_width):
        width = psi.shape[1]
        reach = (tiles.shape[1] - 1) // 2
        beyond = half_width[0] - (reach * width - LANES + 1)
        level = lax.shift_right_arithmetic(beyond, (LANES // LEVELS).bit_length() - 1)
        branches = [functools.partial(rotate, i) for i in range(LEVELS)]
        return lax.switch(level, branches, psi, tiles, half_width)

    return jax.shard_map(
        on_device,
        mesh=mesh,
        in_specs=(P("ga", "band"), P("band", None, "ga", None), P()),
        out_specs=P("ga", "band"),
        check_vma=False,
    )
```

```python
import functools
import math

import jax
import jax.numpy as jnp
from jax import lax
from jax.experimental import pallas as pl
from jax.experimental.pallas import tpu as pltpu
from jax.sharding import PartitionSpec as P

MESH = pl.DeviceIdType.MESH
CHUNKS = 8
EDGE_CHUNKS = 4
LANES = 128
SUB = 256
LEVELS = 16
AHEAD = 1
EDGE_AHEAD = 2


def split(x):
    high = x.astype(jnp.bfloat16)
    return high, (x - high.astype(jnp.float32)).astype(jnp.bfloat16)


def product(x, high, low):
    x_high, x_low = split(x)
    dot = functools.partial(jnp.dot, preferred_element_type=jnp.float32)
    return dot(x_high, high) + (dot(x_high, low) + dot(x_low, high))


def kernel(n, n_ga, plane, edge, hw_ref, psi, tiles, out, own, near, relay, raw, high, low,
           edge_own, edge_near, edge_relay, own_sem, tile_send, tile_recv, send, recv, relay_recv,
           forward_send, edge_send, edge_recv, edge_relay_recv, edge_forward_send):
    me = lax.axis_index("band")
    ga = lax.axis_index("ga")
    rows, width = psi.shape
    span, part = tiles.shape[1], tiles.shape[2]
    reach = (span - 1) // 2
    chunk = rows // CHUNKS
    edge_rows = rows // EDGE_CHUNKS
    sub = math.gcd(chunk, SUB)
    edge_sub = math.gcd(edge_rows, SUB)
    edge_at = (LANES - edge, 0)
    planes = n // plane
    relays = plane >= 4 and planes > 1
    moves = [s * m for m in range(1, reach + 1) for s in (1, -1)]
    at, last = lax.rem(me, plane), lax.div(me, plane)

    peers = []
    for move in moves:
        there = me + move
        peers.append(((there >= 0) & (there < n), there))
        back = me - move
        peers.append(((back >= 0) & (back < n), back))
    up_src = (at == plane - 1) & (last < planes - 1)
    up_mid = (at == 0) & (last < planes - 1)
    up_dst = (at == 0) & (last > 0)
    down_src = (at == 0) & (last > 0)
    down_mid = (at == plane - 2) & (last > 0)
    down_dst = (at == plane - 1) & (last < planes - 1)
    up_mid_of_src = me - (plane - 1)
    down_mid_of_src = me + (plane - 2)
    if relays:
        peers += [
            (up_src, me - (plane - 1)), (up_mid, me + (plane - 1)),
            (up_mid, me + plane), (up_dst, me - plane),
            (down_src, me + (plane - 2)), (down_mid, me - (plane - 2)),
            (down_mid, me - (plane - 1)), (down_dst, me + (plane - 1)),
        ]
    barrier = pltpu.get_barrier_semaphore()
    count = jnp.int32(n_ga - 1)
    for step in range(1, n_ga):
        pl.semaphore_signal(barrier, inc=1, device_id=(me, lax.rem(ga + step, n_ga)), device_id_type=MESH)
    for cond, peer in peers:
        @pl.when(cond)
        def _(peer=peer):
            pl.semaphore_signal(barrier, inc=1, device_id=(peer, ga), device_id_type=MESH)
        count = count + cond.astype(jnp.int32)
    pl.semaphore_wait(barrier, count)

    def block(c):
        return pl.ds(pl.multiple_of(c * chunk, chunk), chunk)

    def columns(slot, move):
        if abs(move) != reach:
            return pl.ds(0, width)
        return pl.ds(LANES if slot % 2 == 0 else 0, width - LANES)

    def direct_copy(slot, move, c):
        at_ = (block(c), columns(slot, move))
        return pltpu.make_async_remote_copy(
            psi.at[at_], near.at[(slot, *at_)], send.at[slot, c], recv.at[slot, c],
            device_id=(me + move, ga), device_id_type=MESH)

    def relay_copy(slot, mid, c):
        at_ = (block(c), columns(slot, moves[slot]))
        return pltpu.make_async_remote_copy(
            psi.at[at_], relay.at[at_], send.at[slot, c], relay_recv.at[c],
            device_id=(mid, ga), device_id_type=MESH)

    def forward_copy(slot, to, c):
        at_ = (block(c), columns(slot, moves[slot]))
        return pltpu.make_async_remote_copy(
            relay.at[at_], near.at[(slot, *at_)], forward_send.at[c], recv.at[slot, c],
            device_id=(to, ga), device_id_type=MESH)

    def edge_direct(side, move, c):
        at_ = pl.ds(edge_at[side], edge)
        return pltpu.make_async_remote_copy(
            edge_own.at[side, c, at_], edge_near.at[side, c, at_],
            edge_send.at[side, c], edge_recv.at[side, c],
            device_id=(me + move, ga), device_id_type=MESH)

    def edge_relayed(side, mid, c):
        at_ = pl.ds(edge_at[side], edge)
        return pltpu.make_async_remote_copy(
            edge_own.at[side, c, at_], edge_relay.at[c, at_],
            edge_send.at[side, c], edge_relay_recv.at[c],
            device_id=(mid, ga), device_id_type=MESH)

    def edge_forward(side, to, c):
        at_ = pl.ds(edge_at[side], edge)
        return pltpu.make_async_remote_copy(
            edge_relay.at[c, at_], edge_near.at[side, c, at_],
            edge_forward_send.at[c], edge_recv.at[side, c],
            device_id=(to, ga), device_id_type=MESH)

    def goes_up(p, c):
        return lax.rem(c, planes) < planes - 1 - p

    def goes_down(p, c):
        return lax.rem(c, planes) < p

    def tile_copy(step):
        peer = lax.rem(ga + step, n_ga)
        return pltpu.make_async_remote_copy(
            tiles.at[0], raw.at[:, pl.ds(pl.multiple_of(ga * part, part), part), :],
            tile_send.at[step - 1], tile_recv.at[step - 1],
            device_id=(me, peer), device_id_type=MESH)

    for step in range(1, n_ga):
        tile_copy(step).start()

    def send_from(slot, move, c, straight, through):
        there = me + move
        valid = (there >= 0) & (there < n)
        if relays and abs(move) == 1:
            src, mid = (up_src, up_mid_of_src) if move == 1 else (down_src, down_mid_of_src)
            via = src & (goes_up(last, c) if move == 1 else goes_down(last, c))

            @pl.when(via)
            def _():
                through(slot, mid, c).start()
            valid = valid & jnp.logical_not(via)

        @pl.when(valid)
        def _():
            straight(slot, move, c).start()

    def start(c, carry):
        for slot, move in enumerate(moves):
            send_from(slot, move, c, direct_copy, relay_copy)
        return carry
    lax.fori_loop(0, CHUNKS, start, 0)

    own_tiles = pltpu.make_async_copy(
        tiles.at[0], raw.at[:, pl.ds(pl.multiple_of(ga * part, part), part), :], own_sem.at[1])
    own_tiles.start()
    own_psi = pltpu.make_async_copy(psi, own, own_sem.at[0])
    own_psi.start()
    own_tiles.wait()
    for step in range(1, n_ga):
        tile_copy(step).wait_recv()
    half = hw_ref[0]
    piece = min(width, 128)
    pieces = width // piece

    def mask(i, carry):
        k, r = lax.div(i, pieces), lax.rem(i, pieces) * piece
        at_ = pl.ds(pl.multiple_of(r, piece), piece)
        row = lax.broadcasted_iota(jnp.int32, (piece, width), 0) + (r + (k - reach) * width)
        col = lax.broadcasted_iota(jnp.int32, (piece, width), 1)
        u = jnp.where(jnp.abs(row - col) <= half, raw[k, at_, :], 0.0)
        high[k, at_, :], low[k, at_, :] = split(u)
        return carry
    lax.fori_loop(0, span * pieces, mask, 0)
    own_psi.wait()

    def within(first, i, size):
        return pl.ds(pl.multiple_of(first + i * size, size), size)

    def turn(c, carry):
        def part_of(i, inner):
            rows_ = within(c * edge_rows, i, edge_sub)
            lanes = within(0, i, edge_sub)
            edge_own[0, c, :, lanes] = jnp.transpose(own[rows_, 0:LANES])
            edge_own[1, c, :, lanes] = jnp.transpose(own[rows_, width - LANES:width])
            if edge < LANES:
                blank = jnp.zeros((LANES - edge, edge_sub), jnp.float32)
                edge_near[0, c, 0:LANES - edge, lanes] = blank
                edge_near[1, c, edge:LANES, lanes] = blank
            return inner
        return lax.fori_loop(0, edge_rows // edge_sub, part_of, carry)
    lax.fori_loop(0, EDGE_CHUNKS, turn, 0)

    def centre(c, carry):
        at_ = within(0, c, sub)
        out[at_, :] = product(own[at_, :], high[reach], low[reach])
        return carry
    lax.fori_loop(0, rows // sub, centre, 0)

    outer = (reach, -reach)

    def edge_start(c, carry):
        for side, move in enumerate(outer):
            send_from(side, move, c, edge_direct, edge_relayed)
        return carry
    lax.fori_loop(0, EDGE_CHUNKS, edge_start, 0)

    def pass_on(c, arrive, forward):
        @pl.when(up_mid & goes_up(last, c))
        def _():
            arrive(0, me, c).wait_recv()
            forward(0, me + plane, c).start()

        @pl.when(down_mid & goes_down(last, c))
        def _():
            arrive(1, me, c).wait_recv()
            forward(1, me - (plane - 1), c).start()

    if relays:
        for c in range(AHEAD):
            pass_on(jnp.int32(c), relay_copy, forward_copy)

    def step(c, carry):
        if relays:
            @pl.when(c + AHEAD < CHUNKS)
            def _():
                pass_on(c + AHEAD, relay_copy, forward_copy)
        for slot, move in enumerate(moves):
            back = me - move

            @pl.when((back >= 0) & (back < n))
            def _():
                direct_copy(slot, move, c).wait_recv()
                k = reach - move
                cols = columns(slot, move)
                cols = slice(cols.start, cols.start + cols.size)

                def add(i, inner):
                    at_ = within(c * chunk, i, sub)
                    out[at_, :] += product(near[slot, at_, cols], high[k, cols, :], low[k, cols, :])
                    return inner
                lax.fori_loop(0, chunk // sub, add, 0)
        return carry
    lax.fori_loop(0, CHUNKS, step, 0)

    if relays and reach == 1:
        for c in range(EDGE_AHEAD):
            pass_on(jnp.int32(c), edge_relayed, edge_forward)

    def edge_step(c, carry):
        if relays and reach == 1:
            @pl.when(c + EDGE_AHEAD < EDGE_CHUNKS)
            def _():
                pass_on(c + EDGE_AHEAD, edge_relayed, edge_forward)
        for side, move in enumerate(outer):
            back = me - move

            @pl.when((back >= 0) & (back < n))
            def _():
                edge_direct(side, move, c).wait_recv()
                k = reach - move
                cols = slice(0, LANES) if side == 0 else slice(width - LANES, width)

                def add(i, inner):
                    at_ = within(c * edge_rows, i, edge_sub)
                    x = jnp.transpose(edge_near[side, c, :, within(0, i, edge_sub)])
                    out[at_, :] += product(x, high[k, cols, :], low[k, cols, :])
                    return inner
                lax.fori_loop(0, edge_rows // edge_sub, add, 0)
        return carry
    lax.fori_loop(0, EDGE_CHUNKS, edge_step, 0)

    def finish(c, carry):
        for slot, move in enumerate(moves):
            there = me + move

            @pl.when((there >= 0) & (there < n))
            def _():
                direct_copy(slot, move, c).wait_send()
        if relays:
            @pl.when((up_mid & goes_up(last, c)) | (down_mid & goes_down(last, c)))
            def _():
                forward_copy(0, me, c).wait_send()
        return carry
    lax.fori_loop(0, CHUNKS, finish, 0)

    def edge_finish(c, carry):
        for side, move in enumerate(outer):
            there = me + move

            @pl.when((there >= 0) & (there < n))
            def _():
                edge_direct(side, move, c).wait_send()
        if relays and reach == 1:
            @pl.when((up_mid & goes_up(last, c)) | (down_mid & goes_down(last, c)))
            def _():
                edge_forward(0, me, c).wait_send()
        return carry
    lax.fori_loop(0, EDGE_CHUNKS, edge_finish, 0)
    for step_ in range(1, n_ga):
        tile_copy(step_).wait_send()


def plane_size(mesh):
    axis = mesh.axis_names.index("band")
    line = mesh.devices.take(0, axis=1 - axis)
    coords = [getattr(d, "coords", None) for d in line]
    if coords[0] is None:
        return len(coords)
    return sum(c[2] == coords[0][2] for c in coords)


def solution(mesh):
    n, n_ga = mesh.shape["band"], mesh.shape["ga"]
    plane = plane_size(mesh)

    def rotate(level, psi, tiles, half_width):
        rows, width = psi.shape
        span = tiles.shape[1]
        sides = span - 1
        edge = LANES * (level + 1) // LEVELS
        f32, bf16 = jnp.float32, jnp.bfloat16
        dma = pltpu.SemaphoreType.DMA
        edge_shape = (EDGE_CHUNKS, LANES, rows // EDGE_CHUNKS)
        return pl.pallas_call(
            functools.partial(kernel, n, n_ga, plane, edge),
            out_shape=pltpu.VMEM((rows, width), f32),
            in_specs=[
                pl.BlockSpec(memory_space=pltpu.SMEM),
                pl.BlockSpec(memory_space=pl.ANY),
                pl.BlockSpec(memory_space=pl.ANY),
            ],
            out_specs=pl.BlockSpec(memory_space=pltpu.VMEM),
            scratch_shapes=[
                pltpu.VMEM((rows, width), f32),
                pltpu.VMEM((sides, rows, width), f32),
                pltpu.VMEM((rows, width), f32),
                pltpu.VMEM((span, width, width), f32),
                pltpu.VMEM((span, width, width), bf16),
                pltpu.VMEM((span, width, width), bf16),
                pltpu.VMEM((2, *edge_shape), f32),
                pltpu.VMEM((2, *edge_shape), f32),
                pltpu.VMEM(edge_shape, f32),
                dma((2,)),
                dma((n_ga - 1,)),
                dma((n_ga - 1,)),
                dma((sides, CHUNKS)),
                dma((sides, CHUNKS)),
                dma((CHUNKS,)),
                dma((CHUNKS,)),
                dma((2, EDGE_CHUNKS)),
                dma((2, EDGE_CHUNKS)),
                dma((EDGE_CHUNKS,)),
                dma((EDGE_CHUNKS,)),
            ],
            compiler_params=pltpu.CompilerParams(
                collective_id=level, has_side_effects=True, vmem_limit_bytes=52 * 2**20),
            name=f"rotate_{edge}",
        )(half_width, psi, tiles)

    def on_device(psi, tiles, half_width):
        width = psi.shape[1]
        reach = (tiles.shape[1] - 1) // 2
        beyond = half_width[0] - (reach * width - LANES + 1)
        level = lax.shift_right_arithmetic(beyond, (LANES // LEVELS).bit_length() - 1)
        branches = [functools.partial(rotate, i) for i in range(LEVELS)]
        return lax.switch(level, branches, psi, tiles, half_width)

    return jax.shard_map(
        on_device,
        mesh=mesh,
        in_specs=(P("ga", "band"), P("band", None, "ga", None), P()),
        out_specs=P("ga", "band"),
        check_vma=False,
    )
```
